32 devices in a mesh: sub: 8 (over y, x, core), rep: 4 (over z).
Axes of the slice: x: 2, y: 2, z: 4, core: 2. Of those that a mesh axis runs over, the one named last changes fastest.
Arguments:
- loads: bfloat16 [64, 256, 1024], P('sub', 'rep'), may hold values from -6 to 6
- operators: bfloat16 [64, 1024, 1024], P('sub'), may hold values from -0.1875 to 0.1875
- owner: int32 [512, 1], P('sub'), may hold values from 0 to 7; in each aligned block of 64 rows (0 to 63, 64 to 127, ...) at most 16 rows name the same one
- dual_block: int32 [512], P('sub'), may hold values from 0 to 15
- scale_index: int32 [16384], P('sub'), may hold values from 0 to 3
- basis: bfloat16 [16384, 1024], P('sub'), may hold values from -0.046875 to 0.046875
- coarse: bfloat16 [1024, 1024], replicated, may hold values from -0.75 to 0.75
Outputs:
- start: float32 [256, 16384], P('rep', 'sub')
- resid: float32 [256, 16384], P('rep', 'sub')
The draws below stay inside these ranges and needn't reach their ends.
Inputs may be any that keep to these rules, and one draw needn't show every extreme that they name: Among the blocks of the subdomains of one index of sub (aligned blocks of 64 rows), no owner is named more than 16 times, a bound that some block reaches.
All inputs are finite; a program needn't handle non-finite values.
Results may differ from the reference program's by a relative error of at most 0.0075.
Values may be sent and summed in bfloat16 or wider, within the bound.
A program may use at most 128 MiB of HBM per device.

```python
import math
import jax
import jax.numpy as jnp
import numpy as np
from jax import lax

L = 1024
BLK = 128
NB = 1024
K = 256
SUB_DEV = 8
OB = 16
BPS = 8
CAP = 16
SUBS = 64
NDUAL = 16384
N_SUB = 8


def plant(values, rng, smallest, top_value):
    place = [jax.random.randint(jax.random.fold_in(rng, axis), (), 0, length) for axis, length in enumerate(values.shape)]
    widest = values.shape.index(max(values.shape))
    beside = place[:widest] + [(place[widest] + 1) % values.shape[widest]] + place[widest + 1:]
    return values.at[tuple(place)].set(smallest).at[tuple(beside)].set(top_value)


def level_of(own_key, extent, shards, smallest, largest):
    factor_of = 1.0
    for axis_at, parts in shards:
        heights = jax.random.uniform(jax.random.fold_in(jax.random.fold_in(own_key, 6), axis_at), (parts,), jnp.float32, smallest / len(shards), largest / len(shards))
        factor_of = factor_of * jnp.repeat(jnp.exp(heights), extent[axis_at] // parts).reshape((-1,) + (1,) * (len(extent) - 1 - axis_at))
    return factor_of


def deal_out(key, own, number, rows, count, top, limit, skew):
    sequence = jax.random.permutation(key, count)
    packed, ordinary = load_shares(count, rows * top, limit, skew, True), load_shares(count, rows * top, limit, skew, False)
    places = jnp.arange(count)

    def named(lengths, rotation):
        used = int((lengths > 0).sum())
        fixed = max(1, used // 4)
        moved = fixed + (places - fixed + rotation * (used - fixed)) % max(1, count - fixed)
        return jnp.zeros((count,), jnp.int32).at[sequence[jnp.where(places < fixed, places, moved)]].set(jnp.asarray(lengths, jnp.int32))

    lengths = jnp.where(number % 4 == 0, named(packed, number // 4), named(ordinary, number - number // 4 - 1))
    mixed = jax.random.permutation(jax.random.fold_in(own, 3), count)
    donor, receiver = mixed[0:count // 2 * 2:2], mixed[1:count // 2 * 2:2]
    margin = jnp.minimum(lengths[donor] - 1, limit - lengths[receiver]) // 2
    margin = jnp.where((donor == sequence[0]) | (receiver == sequence[0]) | (lengths[receiver] == 0), 0, jnp.maximum(margin, 0))
    moved = jax.random.randint(jax.random.fold_in(own, 4), (count // 2,), 0, 1 << 20) % (margin + 1)
    lengths = lengths.at[donor].add(-moved).at[receiver].add(moved)
    items = jnp.searchsorted(jnp.cumsum(lengths), jnp.arange(rows * top), side="right").astype(jnp.int32)
    grid = items.reshape(top, rows).T
    grid = grid[jax.random.permutation(jax.random.fold_in(own, 1), rows)]
    rotation = jax.random.randint(jax.random.fold_in(own, 2), (rows, 1), 0, top)
    return jnp.take_along_axis(grid, (jnp.arange(top)[None, :] + rotation) % top, axis=1)


def load_shares(number_of, total, bound, skew, full):
    weights = [(1 << 20) // math.isqrt(grade ** skew) + 1 for grade in range(1, number_of + 1)]
    largest = bound if full else min(bound, max(-(-total // number_of), total * weights[0] // sum(weights)))
    least = 1 if total - largest >= number_of - 1 else 0
    counts, spare = [largest] + [least] * (number_of - 1), total - largest - least * (number_of - 1)
    while spare > 0:
        candidates = [i for i in range(1, number_of) if counts[i] < largest] or [i for i in range(1, number_of) if counts[i] < bound]
        pool, budget = sum([weights[i] for i in candidates]), spare
        for i in candidates:
            addition = min(bound - counts[i], max(1, budget * weights[i] // pool), spare)
            counts[i] = counts[i] + addition
            spare = spare - addition
    return np.array(counts)


def gaussian(stream_key, extent, deviation, limit, shards=(), kind=jnp.bfloat16):
    result = deviation * jax.random.normal(stream_key, extent, jnp.float32)
    if shards:
        result = result * level_of(stream_key, extent, shards, -0.22, 0.18)
    return jnp.clip(result, -limit, limit).astype(kind)


def setup_inputs(seed: int = 0) -> dict:
    key_of = jax.random.split(jax.random.key(seed), 8)
    loads = gaussian(key_of[0], (SUBS, K, L), 1.0, 6.0, ((0, 8), (1, 4)))
    operators = gaussian(key_of[1], (SUBS, L, L), L ** -0.5, 0.1875, ((0, 8),))
    owner_keys = jax.random.split(jax.random.fold_in(key_of[2], 1), (SUBS * BPS) // (SUB_DEV * BPS))
    owner_turns = jax.random.permutation(jax.random.fold_in(key_of[2], 3), (SUBS * BPS) // (SUB_DEV * BPS))
    owner = jax.vmap(lambda own, number: deal_out(jax.random.fold_in(key_of[2], 2), own, number, SUB_DEV * BPS, N_SUB, 1, CAP, 2))(owner_keys, owner_turns).reshape((SUBS * BPS, 1))
    dual_block = plant(jax.random.randint(key_of[3], (SUBS * BPS,), 0, OB), jax.random.fold_in(key_of[3], 1), 0, OB - 1).astype(jnp.int32)
    scale_index = plant(jax.random.randint(key_of[4], (NDUAL,), 0, 4), jax.random.fold_in(key_of[4], 1), 0, 3).astype(jnp.int32)
    basis = gaussian(key_of[5], (NDUAL, NB), NDUAL ** -0.5, 0.046875, ((0, 8),))
    coarse = gaussian(key_of[6], (NB, NB), (max(1, NB * NB // NDUAL)) ** -0.5, 0.75)
    return {"loads": loads, "operators": operators, "owner": owner, "dual_block": dual_block, "scale_index": scale_index, "basis": basis, "coarse": coarse}


def apply_all(inputs, operators):
    def one(pair):
        return jnp.dot(pair[0], pair[1], preferred_element_type=jnp.float32).astype(jnp.bfloat16)
    return lax.map(one, (inputs, operators))


def to_blocks(values):
    return values.reshape(SUBS, K, BPS, BLK).transpose(0, 2, 1, 3).reshape(SUBS * BPS, K, BLK)


def collect(values, targets, weight):
    blocks = to_blocks(values).astype(jnp.float32)
    total = jnp.zeros((NDUAL // BLK, K, BLK), jnp.float32).at[targets].add(blocks)
    return total.transpose(1, 0, 2).reshape(K, NDUAL) * weight[None, :]


def reference(loads, operators, owner, dual_block, scale_index, basis, coarse):
    targets = (owner[:, 0] * OB + dual_block).astype(jnp.int32)
    weight = 1.0 / (1.0 + scale_index.astype(jnp.float32))
    terms = apply_all(loads, operators)
    dual = collect(terms, targets, weight)
    coeff = jnp.dot(dual.astype(jnp.bfloat16), basis, preferred_element_type=jnp.float32)
    solved = jnp.dot(coeff.astype(jnp.bfloat16), coarse, preferred_element_type=jnp.float32).astype(jnp.bfloat16)
    start = lax.dot_general(solved, basis, (((1,), (1,)), ((), ())), preferred_element_type=jnp.float32)
    start_blocks = start.astype(jnp.bfloat16).reshape(K, NDUAL // BLK, BLK).transpose(1, 0, 2)
    picked = start_blocks[targets]
    local = picked.reshape(SUBS, BPS, K, BLK).transpose(0, 2, 1, 3).reshape(SUBS, K, L)
    again = apply_all(local, operators)
    applied = collect(again, targets, weight)
    return start, dual - applied
```

```python
import functools

import jax
import jax.numpy as jnp
from jax import lax
from jax.experimental import pallas as pl
from jax.experimental.pallas import tpu as pltpu
from jax.sharding import PartitionSpec as P

BLK = 128
FLOWS = 4
MESH = pl.DeviceIdType.MESH
VMEM_LIMIT = 62 * 1024 * 1024


def add_terms(owner_ref, block_ref, s, prod, acc, per_sub, own_blocks):
    for j in range(per_sub):
        row = s * per_sub + j
        g = owner_ref[row] * own_blocks + block_ref[row]
        acc[g] += prod[:, j * BLK : (j + 1) * BLK]


def first_kernel(own_blocks, owner_ref, block_ref, loads_ref, op_ref, out_ref, acc):
    s = pl.program_id(0)

    @pl.when(s == 0)
    def _():
        acc[...] = jnp.zeros_like(acc)

    prod = jnp.dot(loads_ref[0], op_ref[0], preferred_element_type=jnp.float32)
    add_terms(owner_ref, block_ref, s, prod, acc, op_ref.shape[2] // BLK, own_blocks)

    @pl.when(s == pl.num_programs(0) - 1)
    def _():
        out_ref[...] = acc[...].astype(jnp.bfloat16)


def second_kernel(own_blocks, owner_ref, block_ref, all_ref, op_ref, out_ref, acc):
    s = pl.program_id(0)
    per_sub = op_ref.shape[2] // BLK

    @pl.when(s == 0)
    def _():
        acc[...] = jnp.zeros_like(acc)

    picked = []
    for j in range(per_sub):
        row = s * per_sub + j
        picked.append(all_ref[owner_ref[row] * own_blocks + block_ref[row]])
    local = jnp.concatenate(picked, axis=1)
    prod = jnp.dot(local, op_ref[0], preferred_element_type=jnp.float32)
    add_terms(owner_ref, block_ref, s, prod, acc, per_sub, own_blocks)

    @pl.when(s == pl.num_programs(0) - 1)
    def _():
        out_ref[...] = acc[...].astype(jnp.bfloat16)


def local_call(kernel, name, owner, block, x, x_spec, operators, duals, own_blocks, columns):
    subs, rows, _ = operators.shape
    return pl.pallas_call(
        functools.partial(kernel, own_blocks),
        out_shape=jax.ShapeDtypeStruct((duals, columns, BLK), jnp.bfloat16),
        grid_spec=pltpu.PrefetchScalarGridSpec(
            num_scalar_prefetch=2,
            grid=(subs,),
            in_specs=[x_spec, pl.BlockSpec((1, rows, rows), lambda s, *_: (s, 0, 0))],
            out_specs=pl.BlockSpec((duals, columns, BLK), lambda s, *_: (0, 0, 0)),
            scratch_shapes=[pltpu.VMEM((duals, columns, BLK), jnp.float32)],
        ),
        compiler_params=pltpu.CompilerParams(
            dimension_semantics=("arbitrary",), vmem_limit_bytes=VMEM_LIMIT
        ),
        name=name,
    )(owner, block, x, operators)


def flip(me, r, bits):
    out = me
    for b in range(bits):
        if (r >> b) & 1:
            out = out + (1 - 2 * (me // (1 << b) % 2)) * (1 << b)
    return out


def plan(bits, flows):
    rest = list(range(1, bits))
    return [[0] + (rest if f % 2 == 0 else rest[::-1]) for f in range(flows)]


def step_of(r, order):
    for t, b in enumerate(order):
        if (r >> b) & 1:
            return t
    return len(order)


def slot_table(n, order):
    table, done = {}, 0
    for t, b in enumerate(order):
        done |= 1 << b
        for r in range(n):
            if r & done == 0:
                table[(t, r)] = len(table)
    return table


def entry_barrier(me, peers, bits):
    barrier = pltpu.get_barrier_semaphore()
    for r in peers:
        pl.semaphore_signal(
            barrier, inc=1, device_id={"sub": flip(me, r, bits)}, device_id_type=MESH
        )
    pl.semaphore_wait(barrier, len(peers))


def reduce_scatter(n, bits, me, dense, stage, recv, send_sem, recv_sem, per):
    orders = plan(bits, FLOWS)
    tables = [slot_table(n, order) for order in orders]
    sends = []

    def copy_of(f, r, t, src):
        b = orders[f][t]
        slot = tables[f][(t, r ^ (1 << b))]
        return pltpu.make_async_remote_copy(
            src_ref=src,
            dst_ref=recv.at[f, slot],
            send_sem=send_sem.at[f, slot],
            recv_sem=recv_sem.at[f, slot],
            device_id={"sub": flip(me, 1 << b, bits)},
            device_id_type=MESH,
        )

    def total(f, r, steps):
        part = dense[flip(me, r, bits), pl.ds(f * per, per)].astype(jnp.float32)
        for t in range(steps):
            slot = tables[f][(t, r)]
            pltpu.make_async_remote_copy(
                src_ref=recv.at[f, slot],
                dst_ref=recv.at[f, slot],
                send_sem=send_sem.at[f, slot],
                recv_sem=recv_sem.at[f, slot],
                device_id={"sub": flip(me, 1, bits)},
                device_id_type=MESH,
            ).wait_recv()
            part = part + recv[f, slot].astype(jnp.float32)
        return part

    for t in range(bits):
        for f in range(FLOWS):
            b = orders[f][t]
            group = [r for r in range(n) if step_of(r, orders[f]) == t]
            group.sort(key=lambda r: step_of(r ^ (1 << b), orders[f]))
            for r in group:
                if t == 0:
                    src = dense.at[flip(me, r, bits), pl.ds(f * per, per)]
                else:
                    src = stage.at[f, r]
                    stage[f, r] = total(f, r, t).astype(jnp.bfloat16)
                copy = copy_of(f, r, t, src)
                copy.start()
                sends.append(copy)
    return [total(f, 0, bits) for f in range(FLOWS)], sends


def middle_kernel(
    n,
    dense,
    scale,
    basis,
    coarse,
    start_ref,
    dual_ref,
    gat,
    stage,
    recv,
    cpart,
    cgot,
    call,
    dualb,
    send_sem,
    recv_sem,
    csend_sem,
    crecv_sem,
    dsend_sem,
    drecv_sem,
    gsend_sem,
    grecv_sem,
):
    bits = n.bit_length() - 1
    me = lax.axis_index("sub")
    own_blocks, columns = (dense.shape[1], dense.shape[2])
    per = own_blocks // FLOWS
    entry_barrier(me, list(range(1, n)), bits)
    totals, sends = reduce_scatter(
        n, bits, me, dense, stage, recv, send_sem, recv_sem, per
    )
    weight = 1.0 / (1.0 + scale[...].astype(jnp.float32))
    for f in range(FLOWS):
        for i in range(per):
            blk = f * per + i
            part = totals[f][i] * weight[blk : blk + 1, :]
            dual_ref[:, blk * BLK : (blk + 1) * BLK] = part
            dualb[:, blk * BLK : (blk + 1) * BLK] = part.astype(jnp.bfloat16)
    coeff = jnp.dot(dualb[...], basis[...], preferred_element_type=jnp.float32)

    groups, width = (call.shape[0], call.shape[2])
    rows = n // groups
    tall = columns // rows

    def piece(ref, p):
        return ref.at[p // rows, pl.ds(pl.multiple_of(p % rows * tall, tall), tall)]

    for c in range(groups):
        cpart[c] = coeff[:, c * width : (c + 1) * width].astype(jnp.bfloat16)
    out = []
    for r in range(1, n):
        peer = flip(me, r, bits)
        copy = pltpu.make_async_remote_copy(
            src_ref=piece(cpart, peer),
            dst_ref=cgot.at[r],
            send_sem=csend_sem.at[r],
            recv_sem=crecv_sem.at[r],
            device_id={"sub": peer},
            device_id_type=MESH,
        )
        copy.start()
        out.append(copy)
    mine = piece(cpart, me)[...].astype(jnp.float32)
    for r, copy in zip(range(1, n), out):
        copy.wait_recv()
        mine = mine + cgot[r].astype(jnp.float32)
    piece(call, me)[...] = mine.astype(jnp.bfloat16)
    back = []
    for r in range(1, n):
        copy = pltpu.make_async_remote_copy(
            src_ref=piece(call, me),
            dst_ref=piece(call, me),
            send_sem=dsend_sem.at[r],
            recv_sem=drecv_sem.at[r],
            device_id={"sub": flip(me, r, bits)},
            device_id_type=MESH,
        )
        copy.start()
        back.append(copy)
    for copy in back:
        copy.wait_recv()
    solved = jnp.dot(call[0], coarse[0:width], preferred_element_type=jnp.float32)
    for c in range(1, groups):
        solved = solved + jnp.dot(
            call[c], coarse[c * width : (c + 1) * width], preferred_element_type=jnp.float32
        )
    solved = solved.astype(jnp.bfloat16)
    orders = [order[::-1] for order in plan(bits, FLOWS)]

    def gather_copy(f, r, b):
        where = gat.at[flip(me, r, bits), pl.ds(f * per, per)]
        land = r ^ (1 << b)
        return pltpu.make_async_remote_copy(
            src_ref=where,
            dst_ref=where,
            send_sem=gsend_sem.at[f, land],
            recv_sem=grecv_sem.at[f, land],
            device_id={"sub": flip(me, 1 << b, bits)},
            device_id_type=MESH,
        )

    def arrived(f, r):
        where = gat.at[flip(me, r, bits), pl.ds(f * per, per)]
        pltpu.make_async_remote_copy(
            src_ref=where,
            dst_ref=where,
            send_sem=gsend_sem.at[f, r],
            recv_sem=grecv_sem.at[f, r],
            device_id={"sub": flip(me, 1, bits)},
            device_id_type=MESH,
        ).wait_recv()

    for f in range(FLOWS):
        span = slice(f * per * BLK, (f + 1) * per * BLK)
        part = lax.dot_general(
            solved, basis[span], (((1,), (1,)), ((), ())), preferred_element_type=jnp.float32
        )
        start_ref[:, span] = part
        for i in range(per):
            gat[me, f * per + i] = part[:, i * BLK : (i + 1) * BLK].astype(jnp.bfloat16)
        for b in orders[f]:
            copy = gather_copy(f, 0, b)
            copy.start()
            sends.append(copy)
    known = [[] for _ in range(FLOWS)]
    for u in range(bits):
        for f in range(FLOWS):
            b = orders[f][u]
            if u > 0:
                last = 1 << orders[f][u - 1]
                fresh = [last] + [r ^ last for r in known[f]]
                for r in fresh:
                    arrived(f, r)
                known[f] = known[f] + fresh
                for r in known[f]:
                    copy = gather_copy(f, r, b)
                    copy.start()
                    sends.append(copy)
    for f in range(FLOWS):
        last = 1 << orders[f][bits - 1]
        for r in [last] + [r ^ last for r in known[f]]:
            arrived(f, r)
    for copy in sends + out + back:
        copy.wait_send()


def last_kernel(n, dense, scale, dual_ref, resid_ref, stage, recv, send_sem, recv_sem):
    bits = n.bit_length() - 1
    me = lax.axis_index("sub")
    own_blocks = dense.shape[1]
    per = own_blocks // FLOWS
    entry_barrier(me, [1 << b for b in range(bits)], bits)
    totals, sends = reduce_scatter(
        n, bits, me, dense, stage, recv, send_sem, recv_sem, per
    )
    weight = 1.0 / (1.0 + scale[...].astype(jnp.float32))
    for f in range(FLOWS):
        for i in range(per):
            blk = f * per + i
            span = slice(blk * BLK, (blk + 1) * BLK)
            resid_ref[:, span] = dual_ref[:, span] - totals[f][i] * weight[blk : blk + 1, :]
    for copy in sends:
        copy.wait_send()


def per_device(n, loads, operators, owner, dual_block, scale_index, basis, coarse):
    columns = loads.shape[1]
    local_rows = basis.shape[0]
    own_blocks = local_rows // BLK
    duals = n * own_blocks
    owner = owner.reshape(-1)
    scale = scale_index.reshape(own_blocks, BLK)
    per = own_blocks // FLOWS
    dirs = coarse.shape[0]
    vmem = pl.BlockSpec(memory_space=pltpu.VMEM)
    dma = pltpu.SemaphoreType.DMA

    partial = local_call(
        first_kernel,
        "first_local",
        owner,
        dual_block,
        loads,
        pl.BlockSpec((1, columns, loads.shape[2]), lambda s, *_: (s, 0, 0)),
        operators,
        duals,
        own_blocks,
        columns,
    )
    rows = min(n, columns // 16)
    groups = n // rows
    comm = [
        pltpu.VMEM((FLOWS, n, per, columns, BLK), jnp.bfloat16),
        pltpu.VMEM((FLOWS, n - 1, per, columns, BLK), jnp.bfloat16),
    ]
    start, dual, everywhere = pl.pallas_call(
        functools.partial(middle_kernel, n),
        out_shape=(
            jax.ShapeDtypeStruct((columns, local_rows), jnp.float32),
            jax.ShapeDtypeStruct((columns, local_rows), jnp.float32),
            jax.ShapeDtypeStruct((n, own_blocks, columns, BLK), jnp.bfloat16),
        ),
        in_specs=[vmem] * 4,
        out_specs=(vmem, vmem, vmem),
        scratch_shapes=comm
        + [
            pltpu.VMEM((groups, columns, dirs // groups), jnp.bfloat16),
            pltpu.VMEM((n, columns // rows, dirs // groups), jnp.bfloat16),
            pltpu.VMEM((groups, columns, dirs // groups), jnp.bfloat16),
            pltpu.VMEM((columns, local_rows), jnp.bfloat16),
            dma((FLOWS, n - 1)),
            dma((FLOWS, n - 1)),
            dma((n,)),
            dma((n,)),
            dma((n,)),
            dma((n,)),
            dma((FLOWS, n)),
            dma((FLOWS, n)),
        ],
        compiler_params=pltpu.CompilerParams(
            collective_id=0, has_side_effects=True, vmem_limit_bytes=VMEM_LIMIT
        ),
        name="middle",
    )(partial.reshape(n, own_blocks, columns, BLK), scale, basis, coarse)
    again = local_call(
        second_kernel,
        "second_local",
        owner,
        dual_block,
        everywhere.reshape(duals, columns, BLK),
        pl.BlockSpec(
            (duals, columns, BLK), lambda s, *_: (0, 0, 0), pipeline_mode=pl.Buffered(1)
        ),
        operators,
        duals,
        own_blocks,
        columns,
    )
    resid = pl.pallas_call(
        functools.partial(last_kernel, n),
        out_shape=jax.ShapeDtypeStruct((columns, local_rows), jnp.float32),
        in_specs=[vmem] * 3,
        out_specs=vmem,
        scratch_shapes=comm + [dma((FLOWS, n - 1)), dma((FLOWS, n - 1))],
        compiler_params=pltpu.CompilerParams(
            collective_id=1, has_side_effects=True, vmem_limit_bytes=VMEM_LIMIT
        ),
        name="last",
    )(again.reshape(n, own_blocks, columns, BLK), scale, dual)
    return (start, resid)


def solution(mesh):
    return jax.shard_map(
        functools.partial(per_device, mesh.shape["sub"]),
        mesh=mesh,
        in_specs=(
            P("sub", "rep", None),
            P("sub", None, None),
            P("sub", None),
            P("sub"),
            P("sub"),
            P("sub", None),
            P(),
        ),
        out_specs=(P("rep", "sub"), P("rep", "sub")),
        check_vma=False,
    )
```

```python
import functools

import jax
import jax.numpy as jnp
from jax import lax
from jax.experimental import pallas as pl
from jax.experimental.pallas import tpu as pltpu
from jax.sharding import PartitionSpec as P

BLK = 128
FLOWS = 4
MESH = pl.DeviceIdType.MESH
VMEM_LIMIT = 62 * 1024 * 1024
F32 = jnp.float32
BF16 = jnp.bfloat16


def flip(me, r, bits):
    out = me
    for b in range(bits):
        if (r >> b) & 1:
            out = out + (1 - 2 * (me // (1 << b) % 2)) * (1 << b)
    return out


def plan(bits, flows):
    rest = list(range(1, bits))
    return [[0] + (rest if f % 2 == 0 else rest[::-1]) for f in range(flows)]


def step_of(r, order):
    for t, b in enumerate(order):
        if (r >> b) & 1:
            return t
    return len(order)


def slot_table(n, order):
    table, done = {}, 0
    for t, b in enumerate(order):
        done |= 1 << b
        for r in range(n):
            if r & done == 0:
                table[(t, r)] = len(table)
    return table


def reduce_scatter(n, bits, me, local, stage, recv, send_sem, recv_sem):
    orders = plan(bits, FLOWS)
    tables = [slot_table(n, order) for order in orders]
    sends = []

    def copy_of(f, slot, src, b):
        return pltpu.make_async_remote_copy(
            src_ref=src,
            dst_ref=recv.at[f, slot],
            send_sem=send_sem.at[f, slot],
            recv_sem=recv_sem.at[f, slot],
            device_id={"sub": flip(me, 1 << b, bits)},
            device_id_type=MESH,
        )

    def total(f, r, steps):
        part = local(f, flip(me, r, bits))
        for t in range(steps):
            slot = tables[f][(t, r)]
            copy_of(f, slot, recv.at[f, slot], orders[f][t]).wait_recv()
            part = part + recv[f, slot].astype(F32)
        return part

    for t in range(bits):
        group = []
        for f in range(FLOWS):
            for r in range(n):
                if step_of(r, orders[f]) == t:
                    land = r ^ (1 << orders[f][t])
                    group.append((step_of(land, orders[f]), f, r, land))
        for _, f, r, land in sorted(group):
            stage[f, r - 1] = total(f, r, t).astype(BF16)
            copy = copy_of(f, tables[f][(t, land)], stage.at[f, r - 1], orders[f][t])
            copy.start()
            sends.append(copy)
    return sends, lambda f: total(f, 0, bits)


def kernel(
    n,
    target,
    links,
    scale,
    loads_hbm,
    operators_hbm,
    basis_hbm,
    coarse_hbm,
    start_ref,
    resid_ref,
    loads,
    operators,
    basis,
    coarse,
    runs,
    gat,
    stage,
    recv,
    cacc,
    cpart,
    cgot,
    call,
    dual,
    in_sem,
    op_sem,
    send_sem,
    recv_sem,
    csend_sem,
    crecv_sem,
    dsend_sem,
    drecv_sem,
    gsend_sem,
    grecv_sem,
):
    bits = n.bit_length() - 1
    me = lax.axis_index("sub")
    subs, columns, rows_in = loads.shape
    per_sub = rows_in // BLK
    nblocks = subs * per_sub
    own_blocks = gat.shape[0] // n
    per = own_blocks // FLOWS

    barrier = pltpu.get_barrier_semaphore()
    for r in range(1, n):
        pl.semaphore_signal(
            barrier, inc=1, device_id={"sub": flip(me, r, bits)}, device_id_type=MESH
        )
    load_copy = pltpu.make_async_copy(loads_hbm, loads, in_sem.at[0])
    basis_copy = pltpu.make_async_copy(basis_hbm, basis, in_sem.at[1])
    coarse_copy = pltpu.make_async_copy(coarse_hbm, coarse, in_sem.at[2])

    def op_copy(s):
        return pltpu.make_async_copy(operators_hbm.at[s], operators.at[s], op_sem.at[s])

    load_copy.start()
    for s in range(subs):
        op_copy(s).start()
    basis_copy.start()
    coarse_copy.start()
    runs[nblocks] = jnp.zeros((columns, BLK), F32)
    weight = 1.0 / (1.0 + scale[...].astype(F32))
    load_copy.wait()

    def add_runs(s, prod):
        for j in range(per_sub):
            row = s * per_sub + j
            term = prod[:, j * BLK : (j + 1) * BLK].astype(BF16).astype(F32)
            runs[row] = term + runs[links[row]]

    def first(s, carry):
        op_copy(s).wait()
        add_runs(s, jnp.dot(loads[s], operators[s], preferred_element_type=F32))
        return carry

    lax.fori_loop(0, subs, first, 0)

    def local(f, owner):
        base = nblocks + owner * own_blocks + f * per
        return jnp.stack([runs[links[base + i]] for i in range(per)])

    pl.semaphore_wait(barrier, n - 1)
    sends, finish = reduce_scatter(n, bits, me, local, stage, recv, send_sem, recv_sem)
    basis_copy.wait()
    coarse_copy.wait()
    for f in range(FLOWS):
        span = slice(f * per * BLK, (f + 1) * per * BLK)
        part = finish(f)
        pieces = []
        for i in range(per):
            blk = f * per + i
            pieces.append(part[i] * weight[blk : blk + 1, :])
        wide = jnp.concatenate(pieces, axis=1)
        dual[:, span] = wide
        coeff = jnp.dot(wide.astype(BF16), basis[span], preferred_element_type=F32)
        if f == 0:
            cacc[...] = coeff
        else:
            cacc[...] += coeff

    groups, width = (call.shape[0], call.shape[2])
    rows = n // groups
    tall = columns // rows

    def piece(ref, p):
        return ref.at[p // rows, pl.ds(pl.multiple_of(p % rows * tall, tall), tall)]

    for c in range(groups):
        cpart[c] = cacc[:, c * width : (c + 1) * width].astype(BF16)
    out = []
    for r in range(1, n):
        peer = flip(me, r, bits)
        copy = pltpu.make_async_remote_copy(
            src_ref=piece(cpart, peer),
            dst_ref=cgot.at[r],
            send_sem=csend_sem.at[r],
            recv_sem=crecv_sem.at[r],
            device_id={"sub": peer},
            device_id_type=MESH,
        )
        copy.start()
        out.append(copy)
    mine = piece(cpart, me)[...].astype(F32)
    for r, copy in zip(range(1, n), out):
        copy.wait_recv()
        mine = mine + cgot[r].astype(F32)
    piece(call, me)[...] = mine.astype(BF16)
    back = []
    for r in range(1, n):
        copy = pltpu.make_async_remote_copy(
            src_ref=piece(call, me),
            dst_ref=piece(call, me),
            send_sem=dsend_sem.at[r],
            recv_sem=drecv_sem.at[r],
            device_id={"sub": flip(me, r, bits)},
            device_id_type=MESH,
        )
        copy.start()
        back.append(copy)
    for r, copy in zip(range(1, n), back):
        there = piece(call, flip(me, r, bits))
        pltpu.make_async_remote_copy(
            src_ref=there,
            dst_ref=there,
            send_sem=dsend_sem.at[r],
            recv_sem=drecv_sem.at[r],
            device_id={"sub": flip(me, r, bits)},
            device_id_type=MESH,
        ).wait_recv()
    solved = jnp.dot(call[0], coarse[0:width], preferred_element_type=F32)
    for c in range(1, groups):
        solved = solved + jnp.dot(
            call[c], coarse[c * width : (c + 1) * width], preferred_element_type=F32
        )
    solved = solved.astype(BF16)
    orders = [order[::-1] for order in plan(bits, FLOWS)]

    def gather_copy(f, r, b):
        where = gat.at[pl.ds(flip(me, r, bits) * own_blocks + f * per, per)]
        land = r ^ (1 << b)
        return pltpu.make_async_remote_copy(
            src_ref=where,
            dst_ref=where,
            send_sem=gsend_sem.at[f, land],
            recv_sem=grecv_sem.at[f, land],
            device_id={"sub": flip(me, 1 << b, bits)},
            device_id_type=MESH,
        )

    def arrived(f, r):
        where = gat.at[pl.ds(flip(me, r, bits) * own_blocks + f * per, per)]
        pltpu.make_async_remote_copy(
            src_ref=where,
            dst_ref=where,
            send_sem=gsend_sem.at[f, r],
            recv_sem=grecv_sem.at[f, r],
            device_id={"sub": flip(me, 1, bits)},
            device_id_type=MESH,
        ).wait_recv()

    gathers = []
    for f in range(FLOWS):
        span = slice(f * per * BLK, (f + 1) * per * BLK)
        part = lax.dot_general(
            solved, basis[span], (((1,), (1,)), ((), ())), preferred_element_type=F32
        )
        start_ref[:, span] = part
        for i in range(per):
            gat[me * own_blocks + f * per + i] = part[:, i * BLK : (i + 1) * BLK].astype(BF16)
        for b in orders[f]:
            copy = gather_copy(f, 0, b)
            copy.start()
            gathers.append(copy)
    known = [[] for _ in range(FLOWS)]
    for u in range(bits):
        for f in range(FLOWS):
            b = orders[f][u]
            if u > 0:
                last = 1 << orders[f][u - 1]
                fresh = [last] + [r ^ last for r in known[f]]
                for r in fresh:
                    arrived(f, r)
                known[f] = known[f] + fresh
                for r in known[f]:
                    copy = gather_copy(f, r, b)
                    copy.start()
                    gathers.append(copy)
    for copy in sends + out + back:
        copy.wait_send()
    for f in range(FLOWS):
        last = 1 << orders[f][bits - 1]
        for r in [last] + [r ^ last for r in known[f]]:
            arrived(f, r)

    def second(s, carry):
        picked = [gat[target[s * per_sub + j]] for j in range(per_sub)]
        held = jnp.concatenate(picked, axis=1)
        add_runs(s, jnp.dot(held, operators[s], preferred_element_type=F32))
        return carry

    lax.fori_loop(0, subs, second, 0)
    sends, finish = reduce_scatter(n, bits, me, local, stage, recv, send_sem, recv_sem)
    for f in range(FLOWS):
        part = finish(f)
        for i in range(per):
            blk = f * per + i
            span = slice(blk * BLK, (blk + 1) * BLK)
            resid_ref[:, span] = dual[:, span] - part[i] * weight[blk : blk + 1, :]
    for copy in gathers + sends:
        copy.wait_send()


def per_device(n, loads, operators, owner, dual_block, scale_index, basis, coarse):
    subs, columns, rows_in = loads.shape
    local_rows = basis.shape[0]
    own_blocks = local_rows // BLK
    duals = n * own_blocks
    target = owner.reshape(-1) * own_blocks + dual_block
    nblocks = target.shape[0]
    key = jnp.concatenate([target, jnp.arange(duals, dtype=jnp.int32)])
    bound = jnp.minimum(jnp.arange(nblocks + duals, dtype=jnp.int32), nblocks)
    places = jnp.arange(nblocks, dtype=jnp.int32)
    hit = (key[:, None] == target[None, :]) & (places[None, :] < bound[:, None])
    found = jnp.max(jnp.where(hit, places[None, :], -1), axis=1)
    links = jnp.where(found < 0, nblocks, found)
    scale = scale_index.reshape(own_blocks, BLK)
    per = own_blocks // FLOWS
    dirs = coarse.shape[0]
    rows = min(n, columns // 16)
    groups = n // rows
    vmem = pl.BlockSpec(memory_space=pltpu.VMEM)
    smem = pl.BlockSpec(memory_space=pltpu.SMEM)
    hbm = pl.BlockSpec(memory_space=pl.ANY)
    dma = pltpu.SemaphoreType.DMA
    out = jax.ShapeDtypeStruct((columns, local_rows), F32)
    return pl.pallas_call(
        functools.partial(kernel, n),
        out_shape=(out, out),
        in_specs=[smem, smem, vmem] + [hbm] * 4,
        out_specs=(vmem, vmem),
        scratch_shapes=[
            pltpu.VMEM(loads.shape, BF16),
            pltpu.VMEM(operators.shape, BF16),
            pltpu.VMEM(basis.shape, BF16),
            pltpu.VMEM(coarse.shape, BF16),
            pltpu.VMEM((nblocks + 1, columns, BLK), F32),
            pltpu.VMEM((duals, columns, BLK), BF16),
            pltpu.VMEM((FLOWS, n - 1, per, columns, BLK), BF16),
            pltpu.VMEM((FLOWS, n - 1, per, columns, BLK), BF16),
            pltpu.VMEM((columns, dirs), F32),
            pltpu.VMEM((groups, columns, dirs // groups), BF16),
            pltpu.VMEM((n, columns // rows, dirs // groups), BF16),
            pltpu.VMEM((groups, columns, dirs // groups), BF16),
            pltpu.VMEM((columns, local_rows), F32),
            dma((3,)),
            dma((subs,)),
            dma((FLOWS, n - 1)),
            dma((FLOWS, n - 1)),
            dma((n,)),
            dma((n,)),
            dma((n,)),
            dma((n,)),
            dma((FLOWS, n)),
            dma((FLOWS, n)),
        ],
        compiler_params=pltpu.CompilerParams(
            collective_id=0, has_side_effects=True, vmem_limit_bytes=VMEM_LIMIT
        ),
        name="feti",
    )(target, links, scale, loads, operators, basis, coarse)


def solution(mesh):
    return jax.shard_map(
        functools.partial(per_device, mesh.shape["sub"]),
        mesh=mesh,
        in_specs=(
            P("sub", "rep", None),
            P("sub", None, None),
            P("sub", None),
            P("sub"),
            P("sub"),
            P("sub", None),
            P(),
        ),
        out_specs=(P("rep", "sub"), P("rep", "sub")),
        check_vma=False,
    )
```

```python
import functools

import jax
import jax.numpy as jnp
from jax import lax
from jax.experimental import pallas as pl
from jax.experimental.pallas import tpu as pltpu
from jax.sharding import PartitionSpec as P

BLK = 128
FLOWS = 2
GROUPS = 2
PARTS = 2
MESH = pl.DeviceIdType.MESH
VMEM_LIMIT = 62 * 1024 * 1024
F32 = jnp.float32
BF16 = jnp.bfloat16


def flip(me, r, bits):
    out = me
    for b in range(bits):
        if (r >> b) & 1:
            out = out + (1 - 2 * (me // (1 << b) % 2)) * (1 << b)
    return out


def plan(bits, flows):
    rest = list(range(1, bits))
    return [[0] + (rest if f % 2 == 0 else rest[::-1]) for f in range(flows)]


def step_of(r, order):
    for t, b in enumerate(order):
        if (r >> b) & 1:
            return t
    return len(order)


def slot_table(n, order):
    table, done = {}, 0
    for t, b in enumerate(order):
        done |= 1 << b
        for r in range(n):
            if r & done == 0:
                table[(t, r)] = len(table)
    return table


def interleave(pipelines):
    pipelines = list(pipelines)
    while pipelines:
        for one in list(pipelines):
            if next(one, "end") == "end":
                pipelines.remove(one)


def kernel(
    n,
    target,
    links,
    scale,
    loads_hbm,
    operators_hbm,
    basis_hbm,
    coarse_hbm,
    start_ref,
    resid_ref,
    loads,
    operators,
    basis,
    coarse,
    runs,
    gathered,
    stage,
    recv,
    cpart,
    cgot,
    call,
    dual,
    in_sem,
    op_sem,
    send_sem,
    recv_sem,
    csend_sem,
    crecv_sem,
    dsend_sem,
    drecv_sem,
    gsend_sem,
    grecv_sem,
):
    bits = n.bit_length() - 1
    me = lax.axis_index("sub")
    subs, columns, rows_in = loads.shape
    per_sub = rows_in // BLK
    nblocks = subs * per_sub
    own_blocks = gathered[0].shape[0] // n
    per = own_blocks // FLOWS
    height = columns // GROUPS
    orders = plan(bits, FLOWS)
    tables = [slot_table(n, order) for order in orders]
    tall, width = (call.shape[2], call.shape[3])
    across = coarse.shape[0] // width

    barrier = pltpu.get_barrier_semaphore()
    for r in range(1, n):
        pl.semaphore_signal(
            barrier, inc=1, device_id={"sub": flip(me, r, bits)}, device_id_type=MESH
        )
    load_copy = pltpu.make_async_copy(loads_hbm, loads, in_sem.at[0])
    basis_copy = pltpu.make_async_copy(basis_hbm, basis, in_sem.at[1])
    coarse_copy = pltpu.make_async_copy(coarse_hbm, coarse, in_sem.at[2])

    def op_copy(s):
        return pltpu.make_async_copy(operators_hbm.at[s], operators.at[s], op_sem.at[s])

    load_copy.start()
    for s in range(subs):
        op_copy(s).start()
    basis_copy.start()
    coarse_copy.start()
    runs[nblocks] = jnp.zeros((columns, BLK), F32)
    weight = 1.0 / (1.0 + scale[...].astype(F32))
    load_copy.wait()

    def add_runs(s, prod, lines):
        for j in range(per_sub):
            row = s * per_sub + j
            term = prod[:, j * BLK : (j + 1) * BLK].astype(BF16).astype(F32)
            runs[row, lines] = term + runs[links[row], lines]

    def first(s, carry):
        op_copy(s).wait()
        add_runs(s, jnp.dot(loads[s], operators[s], preferred_element_type=F32), slice(None))
        return carry

    lax.fori_loop(0, subs, first, 0)
    pl.semaphore_wait(barrier, n - 1)

    def remote(src, dst, sends, recvs, peer):
        return pltpu.make_async_remote_copy(
            src_ref=src,
            dst_ref=dst,
            send_sem=sends,
            recv_sem=recvs,
            device_id={"sub": peer},
            device_id_type=MESH,
        )

    def group(g):
        lines = slice(g * height, (g + 1) * height)
        gat = gathered[g]
        pending = []

        def go(copy):
            copy.start()
            pending.append(copy)

        def halve_copy(f, slot, src, b):
            return remote(
                src,
                recv.at[g, f, slot],
                send_sem.at[g, f, slot],
                recv_sem.at[g, f, slot],
                flip(me, 1 << b, bits),
            )

        def total(f, r, steps):
            base = nblocks + flip(me, r, bits) * own_blocks + f * per
            part = jnp.stack([runs[links[base + i], lines] for i in range(per)])
            for t in range(steps):
                slot = tables[f][(t, r)]
                halve_copy(f, slot, recv.at[g, f, slot], orders[f][t]).wait_recv()
                part = part + recv[g, f, slot].astype(F32)
            return part

        def halve_step(t):
            todo = []
            for f in range(FLOWS):
                for r in range(n):
                    if step_of(r, orders[f]) == t:
                        land = r ^ (1 << orders[f][t])
                        todo.append((step_of(land, orders[f]), f, r, land))
            for _, f, r, land in sorted(todo):
                stage[g, f, r - 1] = total(f, r, t).astype(BF16)
                go(halve_copy(f, tables[f][(t, land)], stage.at[g, f, r - 1], orders[f][t]))

        def settle():
            for copy in pending:
                copy.wait_send()
            pending.clear()

        for t in range(bits):
            halve_step(t)
            yield
        if g == 0:
            basis_copy.wait()
            coarse_copy.wait()
        wide = []
        for f in range(FLOWS):
            part = total(f, 0, bits)
            for i in range(per):
                blk = f * per + i
                wide.append(part[i] * weight[blk : blk + 1, :])
        wide = jnp.concatenate(wide, axis=1)
        dual[lines] = wide
        coeff = jnp.dot(wide.astype(BF16), basis[...], preferred_element_type=F32)
        for p in range(n):
            top, left = (p // across * tall, p % across * width)
            cpart[g, p] = coeff[top : top + tall, left : left + width].astype(BF16)
        for r in range(1, n):
            peer = flip(me, r, bits)
            go(
                remote(
                    cpart.at[g, peer],
                    cgot.at[g, r - 1],
                    csend_sem.at[g, r - 1],
                    crecv_sem.at[g, r - 1],
                    peer,
                )
            )
        yield
        mine = cpart[g, me].astype(F32)
        for r in range(1, n):
            here = cgot.at[g, r - 1]
            remote(
                here, here, csend_sem.at[g, r - 1], crecv_sem.at[g, r - 1], flip(me, r, bits)
            ).wait_recv()
            mine = mine + cgot[g, r - 1].astype(F32)
        call[g, me] = mine.astype(BF16)

        def spread_copy(r, p):
            there = call.at[g, p]
            return remote(
                there, there, dsend_sem.at[g, r - 1], drecv_sem.at[g, r - 1], flip(me, r, bits)
            )

        for r in range(1, n):
            go(spread_copy(r, me))
        yield
        for r in range(1, n):
            spread_copy(r, flip(me, r, bits)).wait_recv()
        bands = []
        for top in range(0, n, across):
            band = jnp.concatenate([call[g, top + c] for c in range(across)], axis=1)
            bands.append(band if n == across else band.astype(F32))
        whole = bands[0] if n == across else jnp.concatenate(bands, axis=0).astype(BF16)
        solved = jnp.dot(whole, coarse[...], preferred_element_type=F32).astype(BF16)

        def spot(f, r):
            return gat.at[pl.ds(flip(me, r, bits) * own_blocks + f * per, per)]

        def double_copy(f, r, b):
            land = r ^ (1 << b)
            return remote(
                spot(f, r),
                spot(f, r),
                gsend_sem.at[g, f, land - 1],
                grecv_sem.at[g, f, land - 1],
                flip(me, 1 << b, bits),
            )

        def arrived(f, r):
            remote(
                spot(f, r),
                spot(f, r),
                gsend_sem.at[g, f, r - 1],
                grecv_sem.at[g, f, r - 1],
                flip(me, 1, bits),
            ).wait_recv()

        back = [order[::-1] for order in orders]
        for f in range(FLOWS):
            span = slice(f * per * BLK, (f + 1) * per * BLK)
            part = lax.dot_general(
                solved, basis[span], (((1,), (1,)), ((), ())), preferred_element_type=F32
            )
            start_ref[lines, span] = part
            for i in range(per):
                spot_of = me * own_blocks + f * per + i
                gat[spot_of] = part[:, i * BLK : (i + 1) * BLK].astype(BF16)
            for b in back[f]:
                go(double_copy(f, 0, b))
        yield
        known = [[] for _ in range(FLOWS)]
        for u in range(1, bits):
            for f in range(FLOWS):
                last = 1 << back[f][u - 1]
                fresh = [last] + [r ^ last for r in known[f]]
                for r in fresh:
                    arrived(f, r)
                known[f] = known[f] + fresh
                for r in known[f]:
                    go(double_copy(f, r, back[f][u]))
            yield
        for f in range(FLOWS):
            last = 1 << back[f][bits - 1]
            for r in [last] + [r ^ last for r in known[f]]:
                arrived(f, r)

        def second(s, carry):
            picked = [gat[target[s * per_sub + j]] for j in range(per_sub)]
            held = jnp.concatenate(picked, axis=1)
            add_runs(s, jnp.dot(held, operators[s], preferred_element_type=F32), lines)
            return carry

        for part in range(PARTS):
            lax.fori_loop(subs * part // PARTS, subs * (part + 1) // PARTS, second, 0)
            yield
        settle()
        for t in range(bits):
            halve_step(t)
            yield
        for f in range(FLOWS):
            part = total(f, 0, bits)
            for i in range(per):
                blk = f * per + i
                span = slice(blk * BLK, (blk + 1) * BLK)
                resid_ref[lines, span] = dual[lines, span] - part[i] * weight[blk : blk + 1, :]
        settle()

    interleave(group(g) for g in range(GROUPS))


def per_device(n, loads, operators, owner, dual_block, scale_index, basis, coarse):
    subs, columns, rows_in = loads.shape
    local_rows = basis.shape[0]
    own_blocks = local_rows // BLK
    duals = n * own_blocks
    target = owner.reshape(-1) * own_blocks + dual_block
    nblocks = target.shape[0]
    key = jnp.concatenate([target, jnp.arange(duals, dtype=jnp.int32)])
    bound = jnp.minimum(jnp.arange(nblocks + duals, dtype=jnp.int32), nblocks)
    places = jnp.arange(nblocks, dtype=jnp.int32)
    hit = (key[:, None] == target[None, :]) & (places[None, :] < bound[:, None])
    found = jnp.max(jnp.where(hit, places[None, :], -1), axis=1)
    links = jnp.where(found < 0, nblocks, found)
    scale = scale_index.reshape(own_blocks, BLK)
    per = own_blocks // FLOWS
    dirs = coarse.shape[0]
    height = columns // GROUPS
    across = min(n, dirs // BLK)
    piece = (height * across // n, dirs // across)
    vmem = pl.BlockSpec(memory_space=pltpu.VMEM)
    smem = pl.BlockSpec(memory_space=pltpu.SMEM)
    hbm = pl.BlockSpec(memory_space=pl.ANY)
    dma = pltpu.SemaphoreType.DMA
    out = jax.ShapeDtypeStruct((columns, local_rows), F32)
    return pl.pallas_call(
        functools.partial(kernel, n),
        out_shape=(out, out),
        in_specs=[smem, smem, vmem] + [hbm] * 4,
        out_specs=(vmem, vmem),
        scratch_shapes=[
            pltpu.VMEM(loads.shape, BF16),
            pltpu.VMEM(operators.shape, BF16),
            pltpu.VMEM(basis.shape, BF16),
            pltpu.VMEM(coarse.shape, BF16),
            pltpu.VMEM((nblocks + 1, columns, BLK), F32),
            tuple(pltpu.VMEM((duals, height, BLK), BF16) for _ in range(GROUPS)),
            pltpu.VMEM((GROUPS, FLOWS, n - 1, per, height, BLK), BF16),
            pltpu.VMEM((GROUPS, FLOWS, n - 1, per, height, BLK), BF16),
            pltpu.VMEM((GROUPS, n) + piece, BF16),
            pltpu.VMEM((GROUPS, n - 1) + piece, BF16),
            pltpu.VMEM((GROUPS, n) + piece, BF16),
            pltpu.VMEM((columns, local_rows), F32),
            dma((3,)),
            dma((subs,)),
            dma((GROUPS, FLOWS, n - 1)),
            dma((GROUPS, FLOWS, n - 1)),
            dma((GROUPS, n - 1)),
            dma((GROUPS, n - 1)),
            dma((GROUPS, n - 1)),
            dma((GROUPS, n - 1)),
            dma((GROUPS, FLOWS, n - 1)),
            dma((GROUPS, FLOWS, n - 1)),
        ],
        compiler_params=pltpu.CompilerParams(
            collective_id=0, has_side_effects=True, vmem_limit_bytes=VMEM_LIMIT
        ),
        name="feti",
    )(target, links, scale, loads, operators, basis, coarse)


def solution(mesh):
    return jax.shard_map(
        functools.partial(per_device, mesh.shape["sub"]),
        mesh=mesh,
        in_specs=(
            P("sub", "rep", None),
            P("sub", None, None),
            P("sub", None),
            P("sub"),
            P("sub"),
            P("sub", None),
            P(),
        ),
        out_specs=(P("rep", "sub"), P("rep", "sub")),
        check_vma=False,
    )
```

```python
import functools

import jax
import jax.numpy as jnp
from jax import lax
from jax.experimental import pallas as pl
from jax.experimental.pallas import tpu as pltpu
from jax.sharding import PartitionSpec as P

BLK = 128
FLOWS = 4
MESH = pl.DeviceIdType.MESH
VMEM_LIMIT = 62 * 1024 * 1024
F32 = jnp.float32
BF16 = jnp.bfloat16


def flip(me, r, bits):
    out = me
    for b in range(bits):
        if (r >> b) & 1:
            out = out + (1 - 2 * (me // (1 << b) % 2)) * (1 << b)
    return out


def plan(bits, flows):
    rest = list(range(1, bits))
    return [[0] + (rest if f % 2 == 0 else rest[::-1]) for f in range(flows)]


def step_of(r, order):
    for t, b in enumerate(order):
        if (r >> b) & 1:
            return t
    return len(order)


def slot_table(n, order):
    table, done = {}, 0
    for t, b in enumerate(order):
        done |= 1 << b
        for r in range(n):
            if r & done == 0:
                table[(t, r)] = len(table)
    return table


def reduce_scatter(n, bits, me, local, stage, recv, send_sem, recv_sem):
    orders = plan(bits, FLOWS)
    tables = [slot_table(n, order) for order in orders]
    sends = []

    def copy_of(f, slot, src, b):
        return pltpu.make_async_remote_copy(
            src_ref=src,
            dst_ref=recv.at[f, slot],
            send_sem=send_sem.at[f, slot],
            recv_sem=recv_sem.at[f, slot],
            device_id={"sub": flip(me, 1 << b, bits)},
            device_id_type=MESH,
        )

    def total(f, r, steps):
        part = local(f, flip(me, r, bits))
        for t in range(steps):
            slot = tables[f][(t, r)]
            copy_of(f, slot, recv.at[f, slot], orders[f][t]).wait_recv()
            part = part + recv[f, slot].astype(F32)
        return part

    for t in range(bits):
        group = []
        for f in range(FLOWS):
            for r in range(n):
                if step_of(r, orders[f]) == t:
                    land = r ^ (1 << orders[f][t])
                    group.append((step_of(land, orders[f]), f, r, land))
        for _, f, r, land in sorted(group):
            stage[f, r - 1] = total(f, r, t).astype(BF16)
            copy = copy_of(f, tables[f][(t, land)], stage.at[f, r - 1], orders[f][t])
            copy.start()
            sends.append(copy)
    return sends, lambda f: total(f, 0, bits)


def kernel(
    n,
    target,
    links,
    scale,
    loads_hbm,
    operators_hbm,
    basis_hbm,
    coarse_hbm,
    start_ref,
    resid_ref,
    loads,
    operators,
    basis,
    coarse,
    runs,
    gat,
    stage,
    recv,
    cacc,
    cpart,
    cgot,
    call,
    dual,
    in_sem,
    op_sem,
    send_sem,
    recv_sem,
    csend_sem,
    crecv_sem,
    dsend_sem,
    drecv_sem,
    gsend_sem,
    grecv_sem,
):
    bits = n.bit_length() - 1
    me = lax.axis_index("sub")
    subs, columns, rows_in = loads.shape
    per_sub = rows_in // BLK
    nblocks = subs * per_sub
    own_blocks = gat.shape[0] // n
    per = own_blocks // FLOWS

    barrier = pltpu.get_barrier_semaphore()
    for r in range(1, n):
        pl.semaphore_signal(
            barrier, inc=1, device_id={"sub": flip(me, r, bits)}, device_id_type=MESH
        )
    load_copy = pltpu.make_async_copy(loads_hbm, loads, in_sem.at[0])
    basis_copy = pltpu.make_async_copy(basis_hbm, basis, in_sem.at[1])
    coarse_copy = pltpu.make_async_copy(coarse_hbm, coarse, in_sem.at[2])

    def op_copy(s):
        return pltpu.make_async_copy(operators_hbm.at[s], operators.at[s], op_sem.at[s])

    load_copy.start()
    for s in range(subs):
        op_copy(s).start()
    basis_copy.start()
    coarse_copy.start()
    runs[nblocks] = jnp.zeros((columns, BLK), F32)
    weight = 1.0 / (1.0 + scale[...].astype(F32))
    load_copy.wait()

    def add_runs(s, prod):
        for j in range(per_sub):
            row = s * per_sub + j
            term = prod[:, j * BLK : (j + 1) * BLK].astype(BF16).astype(F32)
            runs[row] = term + runs[links[row]]

    def first(s, carry):
        op_copy(s).wait()
        add_runs(s, jnp.dot(loads[s], operators[s], preferred_element_type=F32))
        return carry

    lax.fori_loop(0, subs, first, 0)

    def local(f, owner):
        base = nblocks + owner * own_blocks + f * per
        return jnp.stack([runs[links[base + i]] for i in range(per)])

    pl.semaphore_wait(barrier, n - 1)
    sends, finish = reduce_scatter(n, bits, me, local, stage, recv, send_sem, recv_sem)
    basis_copy.wait()
    coarse_copy.wait()
    for f in range(FLOWS):
        span = slice(f * per * BLK, (f + 1) * per * BLK)
        part = finish(f)
        pieces = []
        for i in range(per):
            blk = f * per + i
            pieces.append(part[i] * weight[blk : blk + 1, :])
        wide = jnp.concatenate(pieces, axis=1)
        dual[:, span] = wide
        coeff = jnp.dot(wide.astype(BF16), basis[span], preferred_element_type=F32)
        if f == 0:
            cacc[...] = coeff
        else:
            cacc[...] += coeff

    groups, width = (call.shape[0], call.shape[2])
    rows = n // groups
    tall = columns // rows

    def piece(ref, p):
        return ref.at[p // rows, pl.ds(pl.multiple_of(p % rows * tall, tall), tall)]

    for c in range(groups):
        cpart[c] = cacc[:, c * width : (c + 1) * width].astype(BF16)
    out = []
    for r in range(1, n):
        peer = flip(me, r, bits)
        copy = pltpu.make_async_remote_copy(
            src_ref=piece(cpart, peer),
            dst_ref=cgot.at[r],
            send_sem=csend_sem.at[r],
            recv_sem=crecv_sem.at[r],
            device_id={"sub": peer},
            device_id_type=MESH,
        )
        copy.start()
        out.append(copy)
    mine = piece(cpart, me)[...].astype(F32)
    for r, copy in zip(range(1, n), out):
        copy.wait_recv()
        mine = mine + cgot[r].astype(F32)
    piece(call, me)[...] = mine.astype(BF16)
    back = []
    for r in range(1, n):
        copy = pltpu.make_async_remote_copy(
            src_ref=piece(call, me),
            dst_ref=piece(call, me),
            send_sem=dsend_sem.at[r],
            recv_sem=drecv_sem.at[r],
            device_id={"sub": flip(me, r, bits)},
            device_id_type=MESH,
        )
        copy.start()
        back.append(copy)
    for r, copy in zip(range(1, n), back):
        there = piece(call, flip(me, r, bits))
        pltpu.make_async_remote_copy(
            src_ref=there,
            dst_ref=there,
            send_sem=dsend_sem.at[r],
            recv_sem=drecv_sem.at[r],
            device_id={"sub": flip(me, r, bits)},
            device_id_type=MESH,
        ).wait_recv()
    solved = jnp.dot(call[0], coarse[0:width], preferred_element_type=F32)
    for c in range(1, groups):
        solved = solved + jnp.dot(
            call[c], coarse[c * width : (c + 1) * width], preferred_element_type=F32
        )
    solved = solved.astype(BF16)
    orders = [order[::-1] for order in plan(bits, FLOWS)]

    def gather_copy(f, r, b):
        where = gat.at[pl.ds(flip(me, r, bits) * own_blocks + f * per, per)]
        land = r ^ (1 << b)
        return pltpu.make_async_remote_copy(
            src_ref=where,
            dst_ref=where,
            send_sem=gsend_sem.at[f, land],
            recv_sem=grecv_sem.at[f, land],
            device_id={"sub": flip(me, 1 << b, bits)},
            device_id_type=MESH,
        )

    def arrived(f, r):
        where = gat.at[pl.ds(flip(me, r, bits) * own_blocks + f * per, per)]
        pltpu.make_async_remote_copy(
            src_ref=where,
            dst_ref=where,
            send_sem=gsend_sem.at[f, r],
            recv_sem=grecv_sem.at[f, r],
            device_id={"sub": flip(me, 1, bits)},
            device_id_type=MESH,
        ).wait_recv()

    gathers = []
    for f in range(FLOWS):
        span = slice(f * per * BLK, (f + 1) * per * BLK)
        part = lax.dot_general(
            solved, basis[span], (((1,), (1,)), ((), ())), preferred_element_type=F32
        )
        start_ref[:, span] = part
        for i in range(per):
            gat[me * own_blocks + f * per + i] = part[:, i * BLK : (i + 1) * BLK].astype(BF16)
        for b in orders[f]:
            copy = gather_copy(f, 0, b)
            copy.start()
            gathers.append(copy)
    known = [[] for _ in range(FLOWS)]
    for u in range(bits):
        for f in range(FLOWS):
            b = orders[f][u]
            if u > 0:
                last = 1 << orders[f][u - 1]
                fresh = [last] + [r ^ last for r in known[f]]
                for r in fresh:
                    arrived(f, r)
                known[f] = known[f] + fresh
                for r in known[f]:
                    copy = gather_copy(f, r, b)
                    copy.start()
                    gathers.append(copy)
    for copy in sends + out + back:
        copy.wait_send()
    for f in range(FLOWS):
        last = 1 << orders[f][bits - 1]
        for r in [last] + [r ^ last for r in known[f]]:
            arrived(f, r)

    def second(s, carry):
        picked = [gat[target[s * per_sub + j]] for j in range(per_sub)]
        held = jnp.concatenate(picked, axis=1)
        add_runs(s, jnp.dot(held, operators[s], preferred_element_type=F32))
        return carry

    lax.fori_loop(0, subs, second, 0)
    sends, finish = reduce_scatter(n, bits, me, local, stage, recv, send_sem, recv_sem)
    for f in range(FLOWS):
        part = finish(f)
        for i in range(per):
            blk = f * per + i
            span = slice(blk * BLK, (blk + 1) * BLK)
            resid_ref[:, span] = dual[:, span] - part[i] * weight[blk : blk + 1, :]
    for copy in gathers + sends:
        copy.wait_send()


def hand_over(start_in, resid_in, start_out, resid_out):
    start_out[...] = start_in[...]
    resid_out[...] = resid_in[...]


def per_device(n, loads, operators, owner, dual_block, scale_index, basis, coarse):
    subs, columns, rows_in = loads.shape
    local_rows = basis.shape[0]
    own_blocks = local_rows // BLK
    duals = n * own_blocks
    target = owner.reshape(-1) * own_blocks + dual_block
    nblocks = target.shape[0]
    key = jnp.concatenate([target, jnp.arange(duals, dtype=jnp.int32)])
    bound = jnp.minimum(jnp.arange(nblocks + duals, dtype=jnp.int32), nblocks)
    places = jnp.arange(nblocks, dtype=jnp.int32)
    hit = (key[:, None] == target[None, :]) & (places[None, :] < bound[:, None])
    found = jnp.max(jnp.where(hit, places[None, :], -1), axis=1)
    links = jnp.where(found < 0, nblocks, found)
    scale = scale_index.reshape(own_blocks, BLK)
    per = own_blocks // FLOWS
    dirs = coarse.shape[0]
    rows = min(n, columns // 16)
    groups = n // rows
    vmem = pl.BlockSpec(memory_space=pltpu.VMEM)
    smem = pl.BlockSpec(memory_space=pltpu.SMEM)
    hbm = pl.BlockSpec(memory_space=pl.ANY)
    dma = pltpu.SemaphoreType.DMA
    out = jax.ShapeDtypeStruct((columns, local_rows), F32)
    results = pl.pallas_call(
        functools.partial(kernel, n),
        out_shape=(out, out),
        in_specs=[smem, smem, vmem] + [hbm] * 4,
        out_specs=(vmem, vmem),
        scratch_shapes=[
            pltpu.VMEM(loads.shape, BF16),
            pltpu.VMEM(operators.shape, BF16),
            pltpu.VMEM(basis.shape, BF16),
            pltpu.VMEM(coarse.shape, BF16),
            pltpu.VMEM((nblocks + 1, columns, BLK), F32),
            pltpu.VMEM((duals, columns, BLK), BF16),
            pltpu.VMEM((FLOWS, n - 1, per, columns, BLK), BF16),
            pltpu.VMEM((FLOWS, n - 1, per, columns, BLK), BF16),
            pltpu.VMEM((columns, dirs), F32),
            pltpu.VMEM((groups, columns, dirs // groups), BF16),
            pltpu.VMEM((n, columns // rows, dirs // groups), BF16),
            pltpu.VMEM((groups, columns, dirs // groups), BF16),
            pltpu.VMEM((columns, local_rows), F32),
            dma((3,)),
            dma((subs,)),
            dma((FLOWS, n - 1)),
            dma((FLOWS, n - 1)),
            dma((n,)),
            dma((n,)),
            dma((n,)),
            dma((n,)),
            dma((FLOWS, n)),
            dma((FLOWS, n)),
        ],
        compiler_params=pltpu.CompilerParams(
            collective_id=0, has_side_effects=True, vmem_limit_bytes=VMEM_LIMIT
        ),
        name="feti",
    )(target, links, scale, loads, operators, basis, coarse)
    tile = pl.BlockSpec((columns // 2, local_rows), lambda i: (i, 0))
    return pl.pallas_call(
        hand_over,
        out_shape=(out, out),
        grid=(2,),
        in_specs=[tile, tile],
        out_specs=(tile, tile),
        name="hand_over",
    )(*results)


def solution(mesh):
    return jax.shard_map(
        functools.partial(per_device, mesh.shape["sub"]),
        mesh=mesh,
        in_specs=(
            P("sub", "rep", None),
            P("sub", None, None),
            P("sub", None),
            P("sub"),
            P("sub"),
            P("sub", None),
            P(),
        ),
        out_specs=(P("rep", "sub"), P("rep", "sub")),
        check_vma=False,
    )
```
